32 devices in a mesh: fsdp: 4 (over x, core), ctx: 2 (over y), tp: 4 (over z).
Axes of the slice: x: 2, y: 2, z: 4, core: 2. Of those that a mesh axis runs over, the one named last changes fastest.
Arguments:
- tokens: bfloat16 [8, 1024, 768], P('fsdp', 'ctx'), may hold values from -6 to 6
- ln1_gain: float32 [768], replicated, may hold values from 0.1 to 1.9
- ln1_bias: float32 [768], replicated, may hold values from -1.75 to 1.75
- qkv_weight: bfloat16 [3, 768, 768], P(None, 'fsdp', 'tp'), may hold values from -0.21875 to 0.21875
- qv_bias: float32 [2, 768], P(None, 'tp'), may hold values from -1.25 to 1.25
- out_weight: bfloat16 [768, 768], P('tp', 'fsdp'), may hold values from -1.25 to 1.25
- out_bias: float32 [768], replicated, may hold values from -1.75 to 1.75
- ln2_gain: float32 [768], replicated, may hold values from 0.1 to 1.9
- ln2_bias: float32 [768], replicated, may hold values from -1.75 to 1.75
- fc_weight: bfloat16 [768, 3072], P('fsdp', 'tp'), may hold values from -0.21875 to 0.21875
- fc_bias: float32 [3072], P('tp'), may hold values from -3 to 3
- proj_weight: bfloat16 [3072, 768], P('tp', 'fsdp'), may hold values from -0.109375 to 0.109375
- proj_bias: float32 [768], replicated, may hold values from -1.75 to 1.75
- block_order: int32 [4], replicated, may hold values from 0 to 3, as said below
- out_grad: bfloat16 [8, 1024, 768], P('fsdp', 'ctx'), may hold values from -6 to 6
Outputs:
- result: bfloat16 [8, 1024, 768], P('fsdp', 'ctx')
- tokens_grad: float32 [8, 1024, 768], P('fsdp', 'ctx')
- ln1_gain_grad: float32 [768], replicated
- ln1_bias_grad: float32 [768], replicated
- qkv_weight_grad: float32 [3, 768, 768], P(None, 'fsdp', 'tp')
- qv_bias_grad: float32 [2, 768], P(None, 'tp')
- out_weight_grad: float32 [768, 768], P('tp', 'fsdp')
- out_bias_grad: float32 [768], replicated
- ln2_gain_grad: float32 [768], replicated
- ln2_bias_grad: float32 [768], replicated
- fc_weight_grad: float32 [768, 3072], P('fsdp', 'tp')
- fc_bias_grad: float32 [3072], P('tp')
- proj_weight_grad: float32 [3072, 768], P('tp', 'fsdp')
- proj_bias_grad: float32 [768], replicated
The draws below stay inside these ranges and needn't reach their ends.
Inputs may be any that keep to these rules, and one draw needn't show every extreme that they name: block_order is a permutation of the 4 block numbers.
All inputs are finite; a program needn't handle non-finite values.
Results may differ from the reference program's by a relative error of at most 0.0099.
Values may be sent and summed in bfloat16 or wider, within the bound.
A program may use at most 192 MiB of HBM per device.

```python
import jax
import jax.numpy as jnp
from jax import lax

D = 768
H = 12
HD = 64
FF = 3072
LENGTH = 1024
NBLK = 4
SEQS = 8


def draw_block_order(key, part):
    return jax.random.permutation(jax.random.fold_in(key, 7), jnp.arange(NBLK, dtype=jnp.int32)).astype(jnp.int32)


def levels(key, shape, shards, low, high):
    def one(dim, blocks):
        heights = jax.random.uniform(jax.random.fold_in(jax.random.fold_in(key, 6), dim), (blocks,), jnp.float32, low / len(shards), high / len(shards))
        return jnp.repeat(jnp.exp(heights), shape[dim] // blocks).reshape((-1,) + (1,) * (len(shape) - dim - 1))

    factor_of = one(*shards[0])
    for cut in shards[1:]:
        factor_of = factor_of * one(*cut)
    return factor_of


def bell_draw(stream_key, shape, width, limit, cuts=(), kind=jnp.bfloat16):
    loudness = levels(stream_key, shape, cuts, -0.22, 0.18) if cuts else 1.0
    drawn = jax.random.normal(stream_key, shape, jnp.float32) * width * loudness
    return jnp.minimum(jnp.maximum(drawn, -limit), limit).astype(kind)


def setup_inputs(seed: int = 0) -> dict:
    key_of = jax.random.split(jax.random.key(seed), 16)
    return {
        "tokens": bell_draw(key_of[0], (SEQS, LENGTH, D), 1.0, 6.0, ((0, 4), (1, 2))),
        "ln1_gain": jnp.clip(1.0 + 0.18 * jax.random.normal(key_of[1], (D,), jnp.float32), 0.1, 1.9),
        "ln1_bias": bell_draw(key_of[2], (D,), 0.3, 1.75, (), jnp.float32),
        "qkv_weight": bell_draw(key_of[3], (3, D, D), D ** -0.5, 0.21875, ((1, 4), (2, 4))),
        "qv_bias": bell_draw(key_of[4], (2, D), 0.2, 1.25, ((1, 4),), jnp.float32),
        "out_weight": bell_draw(key_of[5], (D, D), (D // 32) ** -0.5, 1.25, ((0, 4), (1, 4))),
        "out_bias": bell_draw(key_of[6], (D,), 0.3, 1.75, (), jnp.float32),
        "ln2_gain": jnp.clip(1.0 + 0.18 * jax.random.normal(key_of[7], (D,), jnp.float32), 0.1, 1.9),
        "ln2_bias": bell_draw(key_of[8], (D,), 0.3, 1.75, (), jnp.float32),
        "fc_weight": bell_draw(key_of[9], (D, FF), D ** -0.5, 0.21875, ((0, 4), (1, 4))),
        "fc_bias": bell_draw(key_of[10], (FF,), 0.5, 3.0, ((0, 4),), jnp.float32),
        "proj_weight": bell_draw(key_of[11], (FF, D), FF ** -0.5, 0.109375, ((0, 4), (1, 4))),
        "proj_bias": bell_draw(key_of[12], (D,), 0.3, 1.75, (), jnp.float32),
        "block_order": draw_block_order(jax.random.fold_in(key_of[15], 71), 0),
        "out_grad": bell_draw(key_of[14], (SEQS, LENGTH, D), 1.0, 6.0, ((0, 4), (1, 2))),
    }


@jax.custom_vjp
def low(v):
    return lax.optimization_barrier(v.astype(jnp.bfloat16)).astype(jnp.float32)

@jax.custom_vjp
def low_back(v):
    return v

def low_keep(v):
    return (low(v), None)

def low_pass(kept, grad):
    return (grad,)

def back_keep(v):
    return (v, None)

def back_low(kept, grad):
    return (low(grad),)
low.defvjp(low_keep, low_pass)
low_back.defvjp(back_keep, back_low)
exact_mode = lax.Precision.HIGHEST

def normalize(values, gain, bias):
    centre = lax.optimization_barrier(jnp.mean(values, axis=-1, keepdims=True))
    centred = values - centre
    spread = lax.optimization_barrier(jnp.mean(centred * centred, axis=-1, keepdims=True))
    return centred * lax.rsqrt(spread + 1e-05) * gain + bias

def split_heads(values):
    return values.reshape(LENGTH, H, HD).transpose(1, 0, 2)

def reference(tokens, ln1_gain, ln1_bias, qkv_weight, qv_bias, out_weight, out_bias, ln2_gain, ln2_bias, fc_weight, fc_bias, proj_weight, proj_bias, block_order, out_grad):
    row_ids = jnp.arange(LENGTH, dtype=jnp.int32)
    block_rows = LENGTH // NBLK
    positions = block_order[row_ids // block_rows].astype(jnp.int32) * block_rows + row_ids % block_rows
    visible = positions[None, :] <= positions[:, None]
    params = (ln1_gain.astype(jnp.float32), ln1_bias.astype(jnp.float32), qkv_weight.astype(jnp.float32), qv_bias.astype(jnp.float32), out_weight.astype(jnp.float32), out_bias.astype(jnp.float32), ln2_gain.astype(jnp.float32), ln2_bias.astype(jnp.float32), fc_weight.astype(jnp.float32), fc_bias.astype(jnp.float32), proj_weight.astype(jnp.float32), proj_bias.astype(jnp.float32))

    def one_head(parts):
        query_head, key_head, value_head = parts
        scores = low_back(jnp.dot(query_head, key_head.T, precision=exact_mode) * 0.125)
        scores = jnp.where(visible, scores, -1e+30)
        prob_low = low(jax.nn.softmax(scores, axis=-1))
        return jnp.dot(prob_low, value_head, precision=exact_mode)

    def forward(inputs, gain_one, bias_one, weight_qkv, bias_qv, weight_out, bias_out, gain_two, bias_two, weight_fc, bias_fc, weight_proj, bias_proj):
        act_one = low(normalize(inputs, gain_one, bias_one))
        query = low(low_back(jnp.dot(act_one, weight_qkv[0], precision=exact_mode) + bias_qv[0]))
        key = low(low_back(jnp.dot(act_one, weight_qkv[1], precision=exact_mode)))
        value = low(low_back(jnp.dot(act_one, weight_qkv[2], precision=exact_mode) + bias_qv[1]))
        attended = lax.map(jax.checkpoint(one_head), (split_heads(query), split_heads(key), split_heads(value)))
        mixed = low(low_back(attended.transpose(1, 0, 2).reshape(LENGTH, D)))
        middle = inputs + low_back(jnp.dot(mixed, weight_out, precision=exact_mode) + bias_out)
        act_two = low(normalize(middle, gain_two, bias_two))
        hidden_pre = low_back(jnp.dot(act_two, weight_fc, precision=exact_mode) + bias_fc)
        hidden = low(jax.nn.gelu(hidden_pre, approximate=True))
        return middle + low_back(jnp.dot(hidden, weight_proj, precision=exact_mode) + bias_proj)
    zeros = tuple((jnp.zeros_like(value) for value in params))

    def one_sequence(running, operands):
        sequence_in, sequence_grad = operands
        output, backward = jax.vjp(forward, sequence_in.astype(jnp.float32), *params)
        grads = backward(sequence_grad.astype(jnp.float32))
        updated = tuple((first + second for first, second in zip(running, grads[1:])))
        return (updated, (output.astype(jnp.bfloat16), grads[0]))
    totals, outputs = lax.scan(one_sequence, zeros, (tokens, out_grad))
    result, tokens_grad = outputs
    return (result, tokens_grad, totals[0], totals[1], totals[2], totals[3], totals[4], totals[5], totals[6], totals[7], totals[8], totals[9], totals[10], totals[11])
```

```python
import jax
import jax.numpy as jnp
from jax import lax
from jax.sharding import PartitionSpec as P

HD = 64


def gelu_curve(values):
    return jax.nn.gelu(values, approximate=True)


def normalized(values):
    centre = jnp.mean(values, axis=-1, keepdims=True)
    centred = values - centre
    scale = lax.rsqrt(jnp.mean(centred * centred, axis=-1, keepdims=True) + 1e-05)
    return (centred * scale, scale)


def norm_back(grad_in, gain, normed, scale):
    scaled = grad_in * gain
    return scale * (
        scaled
        - jnp.mean(scaled, axis=-1, keepdims=True)
        - normed * jnp.mean(scaled * normed, axis=-1, keepdims=True)
    )


def swap(values, axis_name, bit):
    count = lax.axis_size(axis_name)
    return lax.ppermute(values, axis_name, [(i, i ^ bit) for i in range(count)])


def sum_all(values, axis_name):
    bit = 1
    while bit < lax.axis_size(axis_name):
        values = values + swap(values, axis_name, bit)
        bit *= 2
    return values


def scatter_rows(values, axis_name):
    count = lax.axis_size(axis_name)
    index = lax.axis_index(axis_name)
    lead, rows, width = values.shape
    values = values.reshape(lead, count, rows // count, width)
    bit = 1
    while bit < count:
        low = (index // bit) % 2
        pairs = values.reshape(lead, values.shape[1] // 2, 2, rows // count, width)
        kept = lax.dynamic_index_in_dim(pairs, low, 2, False)
        given = lax.dynamic_index_in_dim(pairs, 1 - low, 2, False).astype(jnp.bfloat16)
        values = kept + swap(given, axis_name, bit).astype(jnp.float32)
        bit *= 2
    return values[:, 0]


def combine(values):
    low = values.astype(jnp.bfloat16)
    if lax.axis_size("ctx") == 2:
        return low.astype(jnp.float32) + swap(low, "ctx", 1).astype(jnp.float32)
    return lax.psum(low, "ctx").astype(jnp.float32)


def query_side(query_rows, pair_rows, grad_rows, lse_rows, visible):
    columns = query_rows.shape[1]
    heads_here = columns // HD
    length = pair_rows.shape[0]
    query_grad = jnp.zeros(query_rows.shape, jnp.float32)
    delta_cols = jnp.zeros((query_rows.shape[0], heads_here), jnp.float32)
    pair_term = jnp.zeros((length, 2 * columns), jnp.float32)

    def one_head(head_index, running):
        query_grad, pair_term, delta_cols = running
        start = head_index * HD
        query_head = lax.dynamic_slice_in_dim(query_rows, start, HD, 1)
        key_head = lax.dynamic_slice_in_dim(pair_rows, start, HD, 1)
        value_head = lax.dynamic_slice_in_dim(pair_rows, columns + start, HD, 1)
        grad_head = lax.dynamic_slice_in_dim(grad_rows, start, HD, 1)
        lse_head = lax.dynamic_slice_in_dim(lse_rows, head_index, 1, 1)
        scores = (
            jnp.einsum("qd,kd->qk", query_head, key_head, preferred_element_type=jnp.float32)
            * 0.125
        )
        scores = jnp.where(visible, scores, -1e30)
        prob_rows = jnp.exp(scores - lse_head)
        prob_grad = jnp.einsum(
            "qd,kd->qk", grad_head, value_head, preferred_element_type=jnp.float32
        )
        row_delta = jnp.sum(prob_rows * prob_grad, axis=-1, keepdims=True)
        score_grad = (prob_rows * (prob_grad - row_delta)).astype(jnp.bfloat16)
        query_part = (
            jnp.einsum("qk,kd->qd", score_grad, key_head, preferred_element_type=jnp.float32)
            * 0.125
        )
        query_grad = lax.dynamic_update_slice_in_dim(query_grad, query_part, start, 1)
        delta_cols = lax.dynamic_update_slice_in_dim(delta_cols, row_delta, head_index, 1)
        key_part = (
            jnp.einsum("qk,qd->kd", score_grad, query_head, preferred_element_type=jnp.float32)
            * 0.125
        )
        value_part = jnp.einsum(
            "qk,qd->kd",
            prob_rows.astype(jnp.bfloat16),
            grad_head,
            preferred_element_type=jnp.float32,
        )
        pair_term = lax.dynamic_update_slice_in_dim(pair_term, key_part, start, 1)
        pair_term = lax.dynamic_update_slice_in_dim(pair_term, value_part, columns + start, 1)
        return (query_grad, pair_term, delta_cols)

    return lax.fori_loop(0, heads_here, one_head, (query_grad, pair_term, delta_cols))


def body(
    tokens,
    ln1_gain,
    ln1_bias,
    qkv_weight,
    qv_bias,
    out_weight,
    out_bias,
    ln2_gain,
    ln2_bias,
    fc_weight,
    fc_bias,
    proj_weight,
    proj_bias,
    block_order,
    out_grad,
):
    seq_count, seq_rows, model_width = tokens.shape
    ctx_count = lax.axis_size("ctx")
    length = seq_rows * ctx_count
    block_rows = length // (2 * ctx_count)
    all_rows = jnp.arange(length, dtype=jnp.int32)
    slot_ids = jnp.arange(2 * ctx_count, dtype=jnp.int32)
    owner = all_rows[:, None] // block_rows == slot_ids[None, :]
    place_all = (
        jnp.sum(jnp.where(owner, block_order[None, :], 0), axis=1) * block_rows
        + all_rows % block_rows
    )
    place_here = lax.dynamic_slice_in_dim(place_all, lax.axis_index("ctx") * seq_rows, seq_rows)
    visible = place_here[:, None] >= place_all[None, :]
    whole_qkv = lax.all_gather(qkv_weight, "fsdp", axis=1, tiled=True)
    whole_out = lax.all_gather(out_weight.T, "fsdp", axis=0, tiled=True).T
    all_out = lax.all_gather(whole_out, "tp", axis=0, tiled=True)
    whole_fc = lax.all_gather(fc_weight, "fsdp", axis=0, tiled=True)
    proj_flip = lax.all_gather(proj_weight.T, "fsdp", axis=0, tiled=True)
    columns = whole_qkv.shape[-1]
    heads_here = columns // HD
    total_rows = seq_count * seq_rows
    inputs = tokens.reshape(total_rows, model_width).astype(jnp.float32)
    normed_one, scale_one = normalized(inputs)
    act_one = (normed_one * ln1_gain + ln1_bias).astype(jnp.bfloat16)
    proj_qkv = jnp.einsum("td,cdh->cth", act_one, whole_qkv, preferred_element_type=jnp.float32)
    query = (proj_qkv[0] + qv_bias[0]).astype(jnp.bfloat16)
    key = proj_qkv[1].astype(jnp.bfloat16)
    value = (proj_qkv[2] + qv_bias[1]).astype(jnp.bfloat16)
    key_value = jnp.concatenate([key, value], axis=1).reshape(seq_count, seq_rows, 2 * columns)
    pair_whole = lax.all_gather(key_value, "ctx", axis=1, tiled=True)
    query_three = query.reshape(seq_count, seq_rows, columns)
    anchor = jnp.zeros((), jnp.int32)

    def forward_item(counter, running):
        attended, log_sums = running
        sequence = counter // heads_here
        head_index = counter % heads_here
        query_head = lax.dynamic_slice(
            query_three, (sequence, anchor, head_index * HD), (1, seq_rows, HD)
        )[0]
        key_head = lax.dynamic_slice(
            pair_whole, (sequence, anchor, head_index * HD), (1, length, HD)
        )[0]
        value_head = lax.dynamic_slice(
            pair_whole, (sequence, anchor, columns + head_index * HD), (1, length, HD)
        )[0]
        scores = (
            jnp.einsum("qd,kd->qk", query_head, key_head, preferred_element_type=jnp.float32)
            * 0.125
        )
        scores = jnp.where(visible, scores, -1e30)
        row_top = jnp.max(scores, axis=-1, keepdims=True)
        weights = jnp.exp(scores - row_top)
        row_total = jnp.sum(weights, axis=-1, keepdims=True)
        prob_low = (weights / row_total).astype(jnp.bfloat16)
        out_head = jnp.einsum("qk,kd->qd", prob_low, value_head, preferred_element_type=jnp.float32)
        attended = lax.dynamic_update_slice(
            attended, out_head[None], (sequence, anchor, head_index * HD)
        )
        log_sums = lax.dynamic_update_slice(
            log_sums, (row_top + jnp.log(row_total))[None], (sequence, anchor, head_index)
        )
        return (attended, log_sums)

    attended, log_sums = lax.fori_loop(
        0,
        seq_count * heads_here,
        forward_item,
        (
            jnp.zeros((seq_count, seq_rows, columns), jnp.float32),
            jnp.zeros((seq_count, seq_rows, heads_here), jnp.float32),
        ),
    )
    mixed_flip = attended.reshape(total_rows, columns).astype(jnp.bfloat16).T
    all_mixed = lax.all_gather(mixed_flip, "tp", axis=0, tiled=True)
    attn_out = jnp.einsum("ht,hd->td", all_mixed, all_out, preferred_element_type=jnp.float32) + out_bias
    middle = inputs + attn_out
    normed_two, scale_two = normalized(middle)
    act_two = (normed_two * ln2_gain + ln2_bias).astype(jnp.bfloat16)
    hidden_pre = jnp.dot(act_two, whole_fc, preferred_element_type=jnp.float32) + fc_bias
    hidden_out, gelu_back = jax.vjp(gelu_curve, hidden_pre)
    hidden = hidden_out.astype(jnp.bfloat16)
    branch_part = jnp.einsum(
        "tf,df->td", hidden, proj_flip, preferred_element_type=jnp.float32
    ).astype(jnp.bfloat16)
    upstream_low = out_grad.reshape(total_rows, model_width)
    upstream = upstream_low.astype(jnp.float32)
    proj_bias_grad = jnp.sum(upstream, axis=0)
    proj_grad = jnp.einsum("td,tf->df", upstream_low, hidden, preferred_element_type=jnp.float32)
    hidden_grad = jnp.dot(upstream_low, proj_flip, preferred_element_type=jnp.float32)
    pre_grad = gelu_back(hidden_grad)[0].astype(jnp.bfloat16)
    fc_bias_grad = jnp.sum(pre_grad.astype(jnp.float32), axis=0)
    fc_grad = jnp.einsum("td,tf->df", act_two, pre_grad, preferred_element_type=jnp.float32)
    act_two_part = jnp.einsum("tf,df->td", pre_grad, whole_fc, preferred_element_type=jnp.float32)
    ln2_gain_grad = jnp.sum(act_two_part * normed_two, axis=0)
    ln2_bias_grad = jnp.sum(act_two_part, axis=0)
    act_two_grad = lax.psum(act_two_part.astype(jnp.bfloat16), "tp").astype(jnp.float32)
    act_two_grad, branch_part = lax.optimization_barrier((act_two_grad, branch_part))
    branch_low = lax.psum(branch_part, "tp")
    shard_fc = combine(scatter_rows(fc_grad[None], "fsdp"))[0]
    shard_proj = combine(scatter_rows(proj_grad[None], "fsdp"))[0].T
    middle_grad = upstream + norm_back(act_two_grad, ln2_gain, normed_two, scale_two)
    attn_grad = middle_grad.astype(jnp.bfloat16)
    out_bias_grad = jnp.sum(attn_grad.astype(jnp.float32), axis=0)
    out_flip_grad = jnp.einsum("td,ht->dh", attn_grad, mixed_flip, preferred_element_type=jnp.float32)
    shard_out = combine(scatter_rows(out_flip_grad[None], "fsdp"))[0].T
    mixed_grad = (
        jnp.einsum("td,hd->th", attn_grad, whole_out, preferred_element_type=jnp.float32)
        .astype(jnp.bfloat16)
        .reshape(seq_count, seq_rows, columns)
    )
    query_grads = []
    pair_grads = []
    for sequence in range(seq_count):
        query_grad, pair_term, delta_cols = query_side(
            query_three[sequence],
            pair_whole[sequence],
            mixed_grad[sequence],
            log_sums[sequence],
            visible,
        )
        query_grads.append(query_grad)
        pair_grads.append(pair_term)
    query_grad_low = jnp.concatenate(query_grads, axis=0).astype(jnp.bfloat16)
    pair_low = (
        scatter_rows(jnp.stack(pair_grads), "ctx")
        .astype(jnp.bfloat16)
        .reshape(total_rows, 2 * columns)
    )
    stacked = jnp.stack([query_grad_low, pair_low[:, :columns], pair_low[:, columns:]])
    branch_low, stacked = lax.optimization_barrier((branch_low, stacked))
    qv_bias_grad = jnp.stack(
        [
            jnp.sum(stacked[0].astype(jnp.float32), axis=0),
            jnp.sum(stacked[2].astype(jnp.float32), axis=0),
        ]
    )
    qkv_grad = jnp.einsum("td,cth->cdh", act_one, stacked, preferred_element_type=jnp.float32)
    act_one_part = jnp.einsum("cth,cdh->td", stacked, whole_qkv, preferred_element_type=jnp.float32)
    ln1_gain_grad = jnp.sum(act_one_part * normed_one, axis=0)
    ln1_bias_grad = jnp.sum(act_one_part, axis=0)
    act_one_grad = lax.psum(act_one_part.astype(jnp.bfloat16), "tp").astype(jnp.float32)
    shard_qkv = combine(scatter_rows(qkv_grad, "fsdp"))
    norm_sums = sum_all(
        jnp.concatenate([ln1_gain_grad, ln1_bias_grad, ln2_gain_grad, ln2_bias_grad]), "tp"
    )
    packed = jnp.concatenate(
        [norm_sums, out_bias_grad, proj_bias_grad, fc_bias_grad, qv_bias_grad[0], qv_bias_grad[1]]
    )
    packed = sum_all(sum_all(packed, "fsdp"), "ctx")
    hidden_here = fc_bias_grad.shape[0]
    norm_sums = packed[: 6 * model_width].reshape(6, model_width)
    fc_bias_sum = packed[6 * model_width : 6 * model_width + hidden_here]
    qv_sum = packed[6 * model_width + hidden_here :].reshape(2, columns)
    result = (
        (middle + (branch_low.astype(jnp.float32) + proj_bias))
        .astype(jnp.bfloat16)
        .reshape(seq_count, seq_rows, model_width)
    )
    tokens_grad = (middle_grad + norm_back(act_one_grad, ln1_gain, normed_one, scale_one)).reshape(
        seq_count, seq_rows, model_width
    )
    return (
        result,
        tokens_grad,
        norm_sums[0],
        norm_sums[1],
        shard_qkv,
        qv_sum,
        shard_out,
        norm_sums[4],
        norm_sums[2],
        norm_sums[3],
        shard_fc,
        fc_bias_sum,
        shard_proj,
        norm_sums[5],
    )


def solution(mesh):
    in_specs = (
        P("fsdp", "ctx", None),
        P(),
        P(),
        P(None, "fsdp", "tp"),
        P(None, "tp"),
        P("tp", "fsdp"),
        P(),
        P(),
        P(),
        P("fsdp", "tp"),
        P("tp"),
        P("tp", "fsdp"),
        P(),
        P(),
        P("fsdp", "ctx", None),
    )
    out_specs = (
        P("fsdp", "ctx", None),
        P("fsdp", "ctx", None),
        P(),
        P(),
        P(None, "fsdp", "tp"),
        P(None, "tp"),
        P("tp", "fsdp"),
        P(),
        P(),
        P(),
        P("fsdp", "tp"),
        P("tp"),
        P("tp", "fsdp"),
        P(),
    )
    return jax.shard_map(body, mesh=mesh, in_specs=in_specs, out_specs=out_specs, check_vma=False)
```

```python
import jax
import jax.numpy as jnp
from jax import lax
from jax.experimental import pallas as pl
from jax.experimental.pallas import tpu as pltpu
from jax.sharding import PartitionSpec as P

HD = 64


def gelu_curve(values):
    return jax.nn.gelu(values, approximate=True)


def normalized(values):
    centre = jnp.mean(values, axis=-1, keepdims=True)
    centred = values - centre
    scale = lax.rsqrt(jnp.mean(centred * centred, axis=-1, keepdims=True) + 1e-05)
    return (centred * scale, scale)


def norm_back(grad_in, gain, normed, scale):
    scaled = grad_in * gain
    return scale * (
        scaled
        - jnp.mean(scaled, axis=-1, keepdims=True)
        - normed * jnp.mean(scaled * normed, axis=-1, keepdims=True)
    )


def swap(values, axis_name, bit):
    count = lax.axis_size(axis_name)
    return lax.ppermute(values, axis_name, [(i, i ^ bit) for i in range(count)])


def sum_all(values, axis_name):
    bit = 1
    while bit < lax.axis_size(axis_name):
        values = values + swap(values, axis_name, bit)
        bit *= 2
    return values


def scatter_rows(values, axis_name):
    count = lax.axis_size(axis_name)
    index = lax.axis_index(axis_name)
    lead, rows, width = values.shape
    values = values.reshape(lead, count, rows // count, width)
    bit = 1
    while bit < count:
        low = (index // bit) % 2
        pairs = values.reshape(lead, values.shape[1] // 2, 2, rows // count, width)
        kept = lax.dynamic_index_in_dim(pairs, low, 2, False)
        given = lax.dynamic_index_in_dim(pairs, 1 - low, 2, False).astype(jnp.bfloat16)
        values = kept + swap(given, axis_name, bit).astype(jnp.float32)
        bit *= 2
    return values[:, 0]


def combine(values):
    low = values.astype(jnp.bfloat16)
    if lax.axis_size("ctx") == 2:
        return low.astype(jnp.float32) + swap(low, "ctx", 1).astype(jnp.float32)
    return lax.psum(low, "ctx").astype(jnp.float32)


NT = (((1,), (1,)), ((), ()))
NN = (((1,), (0,)), ((), ()))


def dot(left, right, dims=NN):
    return lax.dot_general(left, right, dims, preferred_element_type=jnp.float32)


def flip(values):
    return values.astype(jnp.float32).T.astype(jnp.bfloat16)


def attend_kernel(query_ref, pair_ref, here_ref, all_ref, out_ref, lse_ref):
    columns = query_ref.shape[2]
    visible = here_ref[...] >= all_ref[...]
    for head in range(columns // HD):
        start = head * HD
        query = query_ref[0, :, start : start + HD]
        key = pair_ref[0, :, start : start + HD]
        value = pair_ref[0, :, columns + start : columns + start + HD]
        scores = jnp.where(visible, dot(key, query, NT) * 0.125, -1e30)
        top = jnp.max(scores, axis=0, keepdims=True)
        weights = jnp.exp(scores - top)
        total = jnp.sum(weights, axis=0, keepdims=True)
        prob_low = (weights * (1.0 / total)).astype(jnp.bfloat16)
        out_ref[start : start + HD, :] = dot(flip(value), prob_low).astype(jnp.bfloat16)
        lse_ref[0, head : head + 1, :] = top + jnp.log(total)


def attend(query, pair, place_here, place_all):
    count, rows, columns = query.shape
    length = pair.shape[1]
    heads = columns // HD
    return pl.pallas_call(
        attend_kernel,
        grid=(count,),
        in_specs=[
            pl.BlockSpec((1, rows, columns), lambda s: (s, 0, 0)),
            pl.BlockSpec((1, length, 2 * columns), lambda s: (s, 0, 0)),
            pl.BlockSpec((1, rows), lambda s: (0, 0)),
            pl.BlockSpec((length, 1), lambda s: (0, 0)),
        ],
        out_specs=[
            pl.BlockSpec((columns, rows), lambda s: (0, s)),
            pl.BlockSpec((1, heads, rows), lambda s: (s, 0, 0)),
        ],
        out_shape=[
            jax.ShapeDtypeStruct((columns, count * rows), jnp.bfloat16),
            jax.ShapeDtypeStruct((count, heads, rows), jnp.float32),
        ],
        compiler_params=pltpu.CompilerParams(vmem_limit_bytes=40 * 1024 * 1024),
        cost_estimate=pl.CostEstimate(
            flops=20 * count * rows * length * columns,
            bytes_accessed=count * (rows + 2 * length) * columns * 2,
            transcendentals=count * rows * length * heads,
        ),
        name="attend",
    )(query, pair, place_here[None, :], place_all[:, None])


def attend_back_kernel(
    query_ref, pair_ref, grad_ref, lse_ref, here_ref, all_ref, query_grad_ref, term_ref
):
    columns = query_ref.shape[2]
    visible = here_ref[...] >= all_ref[...]
    query_parts, key_parts, value_parts = [], [], []
    for head in range(columns // HD):
        start = head * HD
        query = query_ref[0, :, start : start + HD]
        key = pair_ref[0, :, start : start + HD]
        value = pair_ref[0, :, columns + start : columns + start + HD]
        grad = grad_ref[0, :, start : start + HD]
        scores = jnp.where(visible, dot(key, query, NT) * 0.125, -1e30)
        prob = jnp.exp(scores - lse_ref[0, head : head + 1, :])
        value_parts.append(dot(prob.astype(jnp.bfloat16), grad))
        weighted = dot(value, grad, NT)
        delta = jnp.sum(prob * weighted, axis=0, keepdims=True)
        score_grad = (prob * (weighted - delta)).astype(jnp.bfloat16)
        key_parts.append(dot(score_grad, query) * 0.125)
        query_parts.append(dot(flip(key), score_grad) * 0.125)
    query_grad_ref[0] = jnp.concatenate(query_parts, axis=0).T.astype(jnp.bfloat16)
    term_ref[0] = jnp.concatenate(key_parts + value_parts, axis=1)


def attend_back(query, pair, grad, lse, place_here, place_all):
    count, rows, columns = query.shape
    length = pair.shape[1]
    heads = columns // HD
    return pl.pallas_call(
        attend_back_kernel,
        grid=(count,),
        in_specs=[
            pl.BlockSpec((1, rows, columns), lambda s: (s, 0, 0)),
            pl.BlockSpec((1, length, 2 * columns), lambda s: (s, 0, 0)),
            pl.BlockSpec((1, rows, columns), lambda s: (s, 0, 0)),
            pl.BlockSpec((1, heads, rows), lambda s: (s, 0, 0)),
            pl.BlockSpec((1, rows), lambda s: (0, 0)),
            pl.BlockSpec((length, 1), lambda s: (0, 0)),
        ],
        out_specs=[
            pl.BlockSpec((1, rows, columns), lambda s: (s, 0, 0)),
            pl.BlockSpec((1, length, 2 * columns), lambda s: (s, 0, 0)),
        ],
        out_shape=[
            jax.ShapeDtypeStruct((count, rows, columns), jnp.bfloat16),
            jax.ShapeDtypeStruct((count, length, 2 * columns), jnp.float32),
        ],
        compiler_params=pltpu.CompilerParams(vmem_limit_bytes=48 * 1024 * 1024),
        cost_estimate=pl.CostEstimate(
            flops=50 * count * rows * length * columns,
            bytes_accessed=count * (2 * rows + 4 * length) * columns * 2,
            transcendentals=count * rows * length * heads,
        ),
        name="attend_back",
    )(query, pair, grad, lse, place_here[None, :], place_all[:, None])


def query_side(query_rows, pair_rows, grad_rows, lse_rows, visible):
    columns = query_rows.shape[1]
    heads_here = columns // HD
    length = pair_rows.shape[0]
    query_grad = jnp.zeros(query_rows.shape, jnp.float32)
    delta_cols = jnp.zeros((query_rows.shape[0], heads_here), jnp.float32)
    pair_term = jnp.zeros((length, 2 * columns), jnp.float32)

    def one_head(head_index, running):
        query_grad, pair_term, delta_cols = running
        start = head_index * HD
        query_head = lax.dynamic_slice_in_dim(query_rows, start, HD, 1)
        key_head = lax.dynamic_slice_in_dim(pair_rows, start, HD, 1)
        value_head = lax.dynamic_slice_in_dim(pair_rows, columns + start, HD, 1)
        grad_head = lax.dynamic_slice_in_dim(grad_rows, start, HD, 1)
        lse_head = lax.dynamic_slice_in_dim(lse_rows, head_index, 1, 1)
        scores = (
            jnp.einsum("qd,kd->qk", query_head, key_head, preferred_element_type=jnp.float32)
            * 0.125
        )
        scores = jnp.where(visible, scores, -1e30)
        prob_rows = jnp.exp(scores - lse_head)
        prob_grad = jnp.einsum(
            "qd,kd->qk", grad_head, value_head, preferred_element_type=jnp.float32
        )
        row_delta = jnp.sum(prob_rows * prob_grad, axis=-1, keepdims=True)
        score_grad = (prob_rows * (prob_grad - row_delta)).astype(jnp.bfloat16)
        query_part = (
            jnp.einsum("qk,kd->qd", score_grad, key_head, preferred_element_type=jnp.float32)
            * 0.125
        )
        query_grad = lax.dynamic_update_slice_in_dim(query_grad, query_part, start, 1)
        delta_cols = lax.dynamic_update_slice_in_dim(delta_cols, row_delta, head_index, 1)
        key_part = (
            jnp.einsum("qk,qd->kd", score_grad, query_head, preferred_element_type=jnp.float32)
            * 0.125
        )
        value_part = jnp.einsum(
            "qk,qd->kd",
            prob_rows.astype(jnp.bfloat16),
            grad_head,
            preferred_element_type=jnp.float32,
        )
        pair_term = lax.dynamic_update_slice_in_dim(pair_term, key_part, start, 1)
        pair_term = lax.dynamic_update_slice_in_dim(pair_term, value_part, columns + start, 1)
        return (query_grad, pair_term, delta_cols)

    return lax.fori_loop(0, heads_here, one_head, (query_grad, pair_term, delta_cols))


def body(
    tokens,
    ln1_gain,
    ln1_bias,
    qkv_weight,
    qv_bias,
    out_weight,
    out_bias,
    ln2_gain,
    ln2_bias,
    fc_weight,
    fc_bias,
    proj_weight,
    proj_bias,
    block_order,
    out_grad,
):
    seq_count, seq_rows, model_width = tokens.shape
    ctx_count = lax.axis_size("ctx")
    length = seq_rows * ctx_count
    block_rows = length // (2 * ctx_count)
    all_rows = jnp.arange(length, dtype=jnp.int32)
    slot_ids = jnp.arange(2 * ctx_count, dtype=jnp.int32)
    owner = all_rows[:, None] // block_rows == slot_ids[None, :]
    place_all = (
        jnp.sum(jnp.where(owner, block_order[None, :], 0), axis=1) * block_rows
        + all_rows % block_rows
    )
    place_here = lax.dynamic_slice_in_dim(place_all, lax.axis_index("ctx") * seq_rows, seq_rows)
    visible = place_here[:, None] >= place_all[None, :]
    whole_qkv = lax.all_gather(qkv_weight, "fsdp", axis=1, tiled=True)
    hidden_cols = fc_weight.shape[1]
    packed_weights = lax.all_gather(
        jnp.concatenate([fc_weight, proj_weight.T, out_weight.T], axis=1), "fsdp", axis=0, tiled=True
    )
    columns = whole_qkv.shape[-1]
    heads_here = columns // HD
    total_rows = seq_count * seq_rows
    inputs = tokens.reshape(total_rows, model_width).astype(jnp.float32)
    normed_one, scale_one = normalized(inputs)
    act_one = (normed_one * ln1_gain + ln1_bias).astype(jnp.bfloat16)
    proj_qkv = jnp.einsum("td,cdh->cth", act_one, whole_qkv, preferred_element_type=jnp.float32)
    query = (proj_qkv[0] + qv_bias[0]).astype(jnp.bfloat16)
    key = proj_qkv[1].astype(jnp.bfloat16)
    value = (proj_qkv[2] + qv_bias[1]).astype(jnp.bfloat16)
    key_value = jnp.concatenate([key, value], axis=1).reshape(seq_count, seq_rows, 2 * columns)
    pair_whole = lax.all_gather(key_value, "ctx", axis=1, tiled=True)
    packed_weights, query = lax.optimization_barrier((packed_weights, query))
    whole_fc = packed_weights[:, :hidden_cols]
    proj_flip = packed_weights[:, hidden_cols : 2 * hidden_cols]
    whole_out = packed_weights[:, 2 * hidden_cols :].T
    all_out = lax.all_gather(whole_out, "tp", axis=0, tiled=True)
    query_three = query.reshape(seq_count, seq_rows, columns)
    anchor = jnp.zeros((), jnp.int32)

    def forward_item(counter, running):
        attended, log_sums = running
        sequence = counter // heads_here
        head_index = counter % heads_here
        query_head = lax.dynamic_slice(
            query_three, (sequence, anchor, head_index * HD), (1, seq_rows, HD)
        )[0]
        key_head = lax.dynamic_slice(
            pair_whole, (sequence, anchor, head_index * HD), (1, length, HD)
        )[0]
        value_head = lax.dynamic_slice(
            pair_whole, (sequence, anchor, columns + head_index * HD), (1, length, HD)
        )[0]
        scores = (
            jnp.einsum("qd,kd->qk", query_head, key_head, preferred_element_type=jnp.float32)
            * 0.125
        )
        scores = jnp.where(visible, scores, -1e30)
        row_top = jnp.max(scores, axis=-1, keepdims=True)
        weights = jnp.exp(scores - row_top)
        row_total = jnp.sum(weights, axis=-1, keepdims=True)
        prob_low = (weights / row_total).astype(jnp.bfloat16)
        out_head = jnp.einsum("qk,kd->qd", prob_low, value_head, preferred_element_type=jnp.float32)
        attended = lax.dynamic_update_slice(
            attended, out_head[None], (sequence, anchor, head_index * HD)
        )
        log_sums = lax.dynamic_update_slice(
            log_sums, (row_top + jnp.log(row_total))[None], (sequence, anchor, head_index)
        )
        return (attended, log_sums)

    in_kernel = length * seq_rows <= 1024 * 1024
    if in_kernel:
        mixed_flip, log_sums = attend(query_three, pair_whole, place_here, place_all)
    else:
        attended, log_sums = lax.fori_loop(
            0,
            seq_count * heads_here,
            forward_item,
            (
                jnp.zeros((seq_count, seq_rows, columns), jnp.float32),
                jnp.zeros((seq_count, seq_rows, heads_here), jnp.float32),
            ),
        )
        mixed_flip = attended.reshape(total_rows, columns).astype(jnp.bfloat16).T
    all_mixed = lax.all_gather(mixed_flip, "tp", axis=0, tiled=True)
    attn_out = jnp.einsum("ht,hd->td", all_mixed, all_out, preferred_element_type=jnp.float32) + out_bias
    middle = inputs + attn_out
    normed_two, scale_two = normalized(middle)
    act_two = (normed_two * ln2_gain + ln2_bias).astype(jnp.bfloat16)
    hidden_pre = jnp.dot(act_two, whole_fc, preferred_element_type=jnp.float32) + fc_bias
    hidden_out, gelu_back = jax.vjp(gelu_curve, hidden_pre)
    hidden = hidden_out.astype(jnp.bfloat16)
    branch_part = jnp.einsum(
        "tf,df->td", hidden, proj_flip, preferred_element_type=jnp.float32
    ).astype(jnp.bfloat16)
    upstream_low = out_grad.reshape(total_rows, model_width)
    upstream = upstream_low.astype(jnp.float32)
    proj_bias_grad = jnp.sum(upstream, axis=0)
    proj_grad = jnp.einsum("td,tf->df", upstream_low, hidden, preferred_element_type=jnp.float32)
    hidden_grad = jnp.dot(upstream_low, proj_flip, preferred_element_type=jnp.float32)
    pre_grad = gelu_back(hidden_grad)[0].astype(jnp.bfloat16)
    fc_bias_grad = jnp.sum(pre_grad.astype(jnp.float32), axis=0)
    fc_grad = jnp.einsum("td,tf->df", act_two, pre_grad, preferred_element_type=jnp.float32)
    act_two_part = jnp.einsum("tf,df->td", pre_grad, whole_fc, preferred_element_type=jnp.float32)
    ln2_gain_grad = jnp.sum(act_two_part * normed_two, axis=0)
    ln2_bias_grad = jnp.sum(act_two_part, axis=0)
    act_two_grad = lax.psum(act_two_part.astype(jnp.bfloat16), "tp").astype(jnp.float32)
    act_two_grad, branch_part = lax.optimization_barrier((act_two_grad, branch_part))
    branch_low = lax.psum(branch_part, "tp")
    shard_fc = combine(scatter_rows(fc_grad[None], "fsdp"))[0]
    shard_proj = combine(scatter_rows(proj_grad[None], "fsdp"))[0].T
    middle_grad = upstream + norm_back(act_two_grad, ln2_gain, normed_two, scale_two)
    attn_grad = middle_grad.astype(jnp.bfloat16)
    out_bias_grad = jnp.sum(attn_grad.astype(jnp.float32), axis=0)
    out_flip_grad = jnp.einsum("td,ht->dh", attn_grad, mixed_flip, preferred_element_type=jnp.float32)
    shard_out = combine(scatter_rows(out_flip_grad[None], "fsdp"))[0].T
    mixed_grad = (
        jnp.einsum("td,hd->th", attn_grad, whole_out, preferred_element_type=jnp.float32)
        .astype(jnp.bfloat16)
        .reshape(seq_count, seq_rows, columns)
    )
    if in_kernel:
        query_grad_low, pair_terms = attend_back(
            query_three, pair_whole, mixed_grad, log_sums, place_here, place_all
        )
        query_grad_low = query_grad_low.reshape(total_rows, columns)
    else:
        query_grads = []
        pair_grads = []
        for sequence in range(seq_count):
            query_grad, pair_term, delta_cols = query_side(
                query_three[sequence],
                pair_whole[sequence],
                mixed_grad[sequence],
                log_sums[sequence],
                visible,
            )
            query_grads.append(query_grad)
            pair_grads.append(pair_term)
        query_grad_low = jnp.concatenate(query_grads, axis=0).astype(jnp.bfloat16)
        pair_terms = jnp.stack(pair_grads)
    pair_low = (
        scatter_rows(pair_terms, "ctx").astype(jnp.bfloat16).reshape(total_rows, 2 * columns)
    )
    stacked = jnp.stack([query_grad_low, pair_low[:, :columns], pair_low[:, columns:]])
    branch_low, stacked = lax.optimization_barrier((branch_low, stacked))
    qv_bias_grad = jnp.stack(
        [
            jnp.sum(stacked[0].astype(jnp.float32), axis=0),
            jnp.sum(stacked[2].astype(jnp.float32), axis=0),
        ]
    )
    qkv_grad = jnp.einsum("td,cth->cdh", act_one, stacked, preferred_element_type=jnp.float32)
    act_one_part = jnp.einsum("cth,cdh->td", stacked, whole_qkv, preferred_element_type=jnp.float32)
    ln1_gain_grad = jnp.sum(act_one_part * normed_one, axis=0)
    ln1_bias_grad = jnp.sum(act_one_part, axis=0)
    act_one_grad = lax.psum(act_one_part.astype(jnp.bfloat16), "tp").astype(jnp.float32)
    shard_qkv = combine(scatter_rows(qkv_grad, "fsdp"))
    norm_sums = sum_all(
        jnp.concatenate([ln1_gain_grad, ln1_bias_grad, ln2_gain_grad, ln2_bias_grad]), "tp"
    )
    packed = jnp.concatenate(
        [norm_sums, out_bias_grad, proj_bias_grad, fc_bias_grad, qv_bias_grad[0], qv_bias_grad[1]]
    )
    packed = sum_all(sum_all(packed, "fsdp"), "ctx")
    result = (
        (middle + (branch_low.astype(jnp.float32) + proj_bias))
        .astype(jnp.bfloat16)
        .reshape(seq_count, seq_rows, model_width)
    )
    act_one_grad, packed, shard_qkv, shard_out = lax.optimization_barrier(
        (act_one_grad, packed, shard_qkv, shard_out)
    )
    tokens_grad = (middle_grad + norm_back(act_one_grad, ln1_gain, normed_one, scale_one)).reshape(
        seq_count, seq_rows, model_width
    )
    hidden_here = fc_bias_grad.shape[0]
    norm_sums = packed[: 6 * model_width].reshape(6, model_width)
    fc_bias_sum = packed[6 * model_width : 6 * model_width + hidden_here]
    qv_sum = packed[6 * model_width + hidden_here :].reshape(2, columns)
    return (
        result,
        tokens_grad,
        norm_sums[0],
        norm_sums[1],
        shard_qkv,
        qv_sum,
        shard_out,
        norm_sums[4],
        norm_sums[2],
        norm_sums[3],
        shard_fc,
        fc_bias_sum,
        shard_proj,
        norm_sums[5],
    )


def solution(mesh):
    in_specs = (
        P("fsdp", "ctx", None),
        P(),
        P(),
        P(None, "fsdp", "tp"),
        P(None, "tp"),
        P("tp", "fsdp"),
        P(),
        P(),
        P(),
        P("fsdp", "tp"),
        P("tp"),
        P("tp", "fsdp"),
        P(),
        P(),
        P("fsdp", "ctx", None),
    )
    out_specs = (
        P("fsdp", "ctx", None),
        P("fsdp", "ctx", None),
        P(),
        P(),
        P(None, "fsdp", "tp"),
        P(None, "tp"),
        P("tp", "fsdp"),
        P(),
        P(),
        P(),
        P("fsdp", "tp"),
        P("tp"),
        P("tp", "fsdp"),
        P(),
    )
    return jax.shard_map(body, mesh=mesh, in_specs=in_specs, out_specs=out_specs, check_vma=False)
```

```python
import jax
import jax.numpy as jnp
from jax import lax
from jax.experimental import pallas as pl
from jax.experimental.pallas import tpu as pltpu
from jax.sharding import PartitionSpec as P

HD = 64


def gelu_curve(values):
    return jax.nn.gelu(values, approximate=True)


def normalized(values):
    centre = jnp.mean(values, axis=-1, keepdims=True)
    centred = values - centre
    scale = lax.rsqrt(jnp.mean(centred * centred, axis=-1, keepdims=True) + 1e-05)
    return (centred * scale, scale)


def norm_back(grad_in, gain, normed, scale):
    scaled = grad_in * gain
    return scale * (
        scaled
        - jnp.mean(scaled, axis=-1, keepdims=True)
        - normed * jnp.mean(scaled * normed, axis=-1, keepdims=True)
    )


def swap(values, axis_name, bit):
    count = lax.axis_size(axis_name)
    return lax.ppermute(values, axis_name, [(i, i ^ bit) for i in range(count)])


def sum_all(values, axis_name):
    bit = 1
    while bit < lax.axis_size(axis_name):
        values = values + swap(values, axis_name, bit)
        bit *= 2
    return values


def scatter_rows(values, axis_name):
    count = lax.axis_size(axis_name)
    index = lax.axis_index(axis_name)
    lead, rows, width = values.shape
    values = values.reshape(lead, count, rows // count, width)
    bit = 1
    while bit < count:
        low = (index // bit) % 2
        pairs = values.reshape(lead, values.shape[1] // 2, 2, rows // count, width)
        kept = lax.dynamic_index_in_dim(pairs, low, 2, False)
        given = lax.dynamic_index_in_dim(pairs, 1 - low, 2, False).astype(jnp.bfloat16)
        values = kept + swap(given, axis_name, bit).astype(jnp.float32)
        bit *= 2
    return values[:, 0]


def combine(values):
    low = values.astype(jnp.bfloat16)
    if lax.axis_size("ctx") == 2:
        return low.astype(jnp.float32) + swap(low, "ctx", 1).astype(jnp.float32)
    return lax.psum(low, "ctx").astype(jnp.float32)


NT = (((1,), (1,)), ((), ()))
NN = (((1,), (0,)), ((), ()))


def dot(left, right, dims=NN):
    return lax.dot_general(left, right, dims, preferred_element_type=jnp.float32)


def flip(values):
    return values.astype(jnp.float32).T.astype(jnp.bfloat16)


def attend_kernel(query_ref, pair_ref, here_ref, all_ref, out_ref, lse_ref):
    columns = query_ref.shape[2]
    visible = here_ref[...] >= all_ref[...]
    for head in range(columns // HD):
        start = head * HD
        query = query_ref[0, :, start : start + HD]
        key = pair_ref[0, :, start : start + HD]
        value = pair_ref[0, :, columns + start : columns + start + HD]
        scores = jnp.where(visible, dot(key, query, NT) * 0.125, -1e30)
        top = jnp.max(scores, axis=0, keepdims=True)
        weights = jnp.exp(scores - top)
        total = jnp.sum(weights, axis=0, keepdims=True)
        prob_low = (weights * (1.0 / total)).astype(jnp.bfloat16)
        out_ref[start : start + HD, :] = dot(flip(value), prob_low).astype(jnp.bfloat16)
        lse_ref[0, head : head + 1, :] = top + jnp.log(total)


def attend(query, pair, place_here, place_all):
    count, rows, columns = query.shape
    length = pair.shape[1]
    heads = columns // HD
    return pl.pallas_call(
        attend_kernel,
        grid=(count,),
        in_specs=[
            pl.BlockSpec((1, rows, columns), lambda s: (s, 0, 0)),
            pl.BlockSpec((1, length, 2 * columns), lambda s: (s, 0, 0)),
            pl.BlockSpec((1, rows), lambda s: (0, 0)),
            pl.BlockSpec((length, 1), lambda s: (0, 0)),
        ],
        out_specs=[
            pl.BlockSpec((columns, rows), lambda s: (0, s)),
            pl.BlockSpec((1, heads, rows), lambda s: (s, 0, 0)),
        ],
        out_shape=[
            jax.ShapeDtypeStruct((columns, count * rows), jnp.bfloat16),
            jax.ShapeDtypeStruct((count, heads, rows), jnp.float32),
        ],
        compiler_params=pltpu.CompilerParams(vmem_limit_bytes=40 * 1024 * 1024),
        cost_estimate=pl.CostEstimate(
            flops=20 * count * rows * length * columns,
            bytes_accessed=count * (rows + 2 * length) * columns * 2,
            transcendentals=count * rows * length * heads,
        ),
        name="attend",
    )(query, pair, place_here[None, :], place_all[:, None])


def attend_back_kernel(
    query_ref, pair_ref, grad_ref, lse_ref, here_ref, all_ref, query_grad_ref, term_ref
):
    columns = query_ref.shape[2]
    visible = here_ref[...] >= all_ref[...]
    query_parts, key_parts, value_parts = [], [], []
    for head in range(columns // HD):
        start = head * HD
        query = query_ref[0, :, start : start + HD]
        key = pair_ref[0, :, start : start + HD]
        value = pair_ref[0, :, columns + start : columns + start + HD]
        grad = grad_ref[0, :, start : start + HD]
        scores = jnp.where(visible, dot(key, query, NT) * 0.125, -1e30)
        prob = jnp.exp(scores - lse_ref[0, head : head + 1, :])
        value_parts.append(dot(prob.astype(jnp.bfloat16), grad))
        weighted = dot(value, grad, NT)
        delta = jnp.sum(prob * weighted, axis=0, keepdims=True)
        score_grad = (prob * (weighted - delta)).astype(jnp.bfloat16)
        key_parts.append(dot(score_grad, query) * 0.125)
        query_parts.append(dot(flip(key), score_grad) * 0.125)
    query_grad_ref[0] = jnp.concatenate(query_parts, axis=0).T.astype(jnp.bfloat16)
    term_ref[0] = jnp.concatenate(key_parts + value_parts, axis=1)


def attend_back(query, pair, grad, lse, place_here, place_all):
    count, rows, columns = query.shape
    length = pair.shape[1]
    heads = columns // HD
    return pl.pallas_call(
        attend_back_kernel,
        grid=(count,),
        in_specs=[
            pl.BlockSpec((1, rows, columns), lambda s: (s, 0, 0)),
            pl.BlockSpec((1, length, 2 * columns), lambda s: (s, 0, 0)),
            pl.BlockSpec((1, rows, columns), lambda s: (s, 0, 0)),
            pl.BlockSpec((1, heads, rows), lambda s: (s, 0, 0)),
            pl.BlockSpec((1, rows), lambda s: (0, 0)),
            pl.BlockSpec((length, 1), lambda s: (0, 0)),
        ],
        out_specs=[
            pl.BlockSpec((1, rows, columns), lambda s: (s, 0, 0)),
            pl.BlockSpec((1, length, 2 * columns), lambda s: (s, 0, 0)),
        ],
        out_shape=[
            jax.ShapeDtypeStruct((count, rows, columns), jnp.bfloat16),
            jax.ShapeDtypeStruct((count, length, 2 * columns), jnp.float32),
        ],
        compiler_params=pltpu.CompilerParams(vmem_limit_bytes=48 * 1024 * 1024),
        cost_estimate=pl.CostEstimate(
            flops=50 * count * rows * length * columns,
            bytes_accessed=count * (2 * rows + 4 * length) * columns * 2,
            transcendentals=count * rows * length * heads,
        ),
        name="attend_back",
    )(query, pair, grad, lse, place_here[None, :], place_all[:, None])


def query_side(query_rows, pair_rows, grad_rows, lse_rows, visible):
    columns = query_rows.shape[1]
    heads_here = columns // HD
    length = pair_rows.shape[0]
    query_grad = jnp.zeros(query_rows.shape, jnp.float32)
    delta_cols = jnp.zeros((query_rows.shape[0], heads_here), jnp.float32)
    pair_term = jnp.zeros((length, 2 * columns), jnp.float32)

    def one_head(head_index, running):
        query_grad, pair_term, delta_cols = running
        start = head_index * HD
        query_head = lax.dynamic_slice_in_dim(query_rows, start, HD, 1)
        key_head = lax.dynamic_slice_in_dim(pair_rows, start, HD, 1)
        value_head = lax.dynamic_slice_in_dim(pair_rows, columns + start, HD, 1)
        grad_head = lax.dynamic_slice_in_dim(grad_rows, start, HD, 1)
        lse_head = lax.dynamic_slice_in_dim(lse_rows, head_index, 1, 1)
        scores = (
            jnp.einsum("qd,kd->qk", query_head, key_head, preferred_element_type=jnp.float32)
            * 0.125
        )
        scores = jnp.where(visible, scores, -1e30)
        prob_rows = jnp.exp(scores - lse_head)
        prob_grad = jnp.einsum(
            "qd,kd->qk", grad_head, value_head, preferred_element_type=jnp.float32
        )
        row_delta = jnp.sum(prob_rows * prob_grad, axis=-1, keepdims=True)
        score_grad = (prob_rows * (prob_grad - row_delta)).astype(jnp.bfloat16)
        query_part = (
            jnp.einsum("qk,kd->qd", score_grad, key_head, preferred_element_type=jnp.float32)
            * 0.125
        )
        query_grad = lax.dynamic_update_slice_in_dim(query_grad, query_part, start, 1)
        delta_cols = lax.dynamic_update_slice_in_dim(delta_cols, row_delta, head_index, 1)
        key_part = (
            jnp.einsum("qk,qd->kd", score_grad, query_head, preferred_element_type=jnp.float32)
            * 0.125
        )
        value_part = jnp.einsum(
            "qk,qd->kd",
            prob_rows.astype(jnp.bfloat16),
            grad_head,
            preferred_element_type=jnp.float32,
        )
        pair_term = lax.dynamic_update_slice_in_dim(pair_term, key_part, start, 1)
        pair_term = lax.dynamic_update_slice_in_dim(pair_term, value_part, columns + start, 1)
        return (query_grad, pair_term, delta_cols)

    return lax.fori_loop(0, heads_here, one_head, (query_grad, pair_term, delta_cols))


def body(
    tokens,
    ln1_gain,
    ln1_bias,
    qkv_weight,
    qv_bias,
    out_weight,
    out_bias,
    ln2_gain,
    ln2_bias,
    fc_weight,
    fc_bias,
    proj_weight,
    proj_bias,
    block_order,
    out_grad,
):
    seq_count, seq_rows, model_width = tokens.shape
    ctx_count = lax.axis_size("ctx")
    length = seq_rows * ctx_count
    block_rows = length // (2 * ctx_count)
    all_rows = jnp.arange(length, dtype=jnp.int32)
    slot_ids = jnp.arange(2 * ctx_count, dtype=jnp.int32)
    owner = all_rows[:, None] // block_rows == slot_ids[None, :]
    place_all = (
        jnp.sum(jnp.where(owner, block_order[None, :], 0), axis=1) * block_rows
        + all_rows % block_rows
    )
    place_here = lax.dynamic_slice_in_dim(place_all, lax.axis_index("ctx") * seq_rows, seq_rows)
    visible = place_here[:, None] >= place_all[None, :]
    whole_qkv = lax.all_gather(qkv_weight, "fsdp", axis=1, tiled=True)
    hidden_cols = fc_weight.shape[1]
    packed_weights = lax.all_gather(
        jnp.concatenate([fc_weight, proj_weight.T, out_weight.T], axis=1), "fsdp", axis=0, tiled=True
    )
    columns = whole_qkv.shape[-1]
    heads_here = columns // HD
    total_rows = seq_count * seq_rows
    inputs = tokens.reshape(total_rows, model_width).astype(jnp.float32)
    normed_one, scale_one = normalized(inputs)
    act_one = (normed_one * ln1_gain + ln1_bias).astype(jnp.bfloat16)
    proj_qkv = jnp.einsum("td,cdh->cth", act_one, whole_qkv, preferred_element_type=jnp.float32)
    query = (proj_qkv[0] + qv_bias[0]).astype(jnp.bfloat16)
    key = proj_qkv[1].astype(jnp.bfloat16)
    value = (proj_qkv[2] + qv_bias[1]).astype(jnp.bfloat16)
    key_value = jnp.concatenate([key, value], axis=1).reshape(seq_count, seq_rows, 2 * columns)
    exchanged = ctx_count == 2
    if exchanged:
        pair_whole = jnp.concatenate([key_value, swap(key_value, "ctx", 1)], axis=1)
        place_there = lax.dynamic_slice_in_dim(
            place_all, (1 - lax.axis_index("ctx")) * seq_rows, seq_rows
        )
        place_all = jnp.concatenate([place_here, place_there])
        visible = place_here[:, None] >= place_all[None, :]
    else:
        pair_whole = lax.all_gather(key_value, "ctx", axis=1, tiled=True)
    packed_weights, query = lax.optimization_barrier((packed_weights, query))
    whole_fc = packed_weights[:, :hidden_cols]
    proj_flip = packed_weights[:, hidden_cols : 2 * hidden_cols]
    whole_out = packed_weights[:, 2 * hidden_cols :].T
    all_out = lax.all_gather(whole_out, "tp", axis=0, tiled=True)
    query_three = query.reshape(seq_count, seq_rows, columns)
    anchor = jnp.zeros((), jnp.int32)

    def forward_item(counter, running):
        attended, log_sums = running
        sequence = counter // heads_here
        head_index = counter % heads_here
        query_head = lax.dynamic_slice(
            query_three, (sequence, anchor, head_index * HD), (1, seq_rows, HD)
        )[0]
        key_head = lax.dynamic_slice(
            pair_whole, (sequence, anchor, head_index * HD), (1, length, HD)
        )[0]
        value_head = lax.dynamic_slice(
            pair_whole, (sequence, anchor, columns + head_index * HD), (1, length, HD)
        )[0]
        scores = (
            jnp.einsum("qd,kd->qk", query_head, key_head, preferred_element_type=jnp.float32)
            * 0.125
        )
        scores = jnp.where(visible, scores, -1e30)
        row_top = jnp.max(scores, axis=-1, keepdims=True)
        weights = jnp.exp(scores - row_top)
        row_total = jnp.sum(weights, axis=-1, keepdims=True)
        prob_low = (weights / row_total).astype(jnp.bfloat16)
        out_head = jnp.einsum("qk,kd->qd", prob_low, value_head, preferred_element_type=jnp.float32)
        attended = lax.dynamic_update_slice(
            attended, out_head[None], (sequence, anchor, head_index * HD)
        )
        log_sums = lax.dynamic_update_slice(
            log_sums, (row_top + jnp.log(row_total))[None], (sequence, anchor, head_index)
        )
        return (attended, log_sums)

    in_kernel = length * seq_rows <= 1024 * 1024
    if in_kernel:
        mixed_flip, log_sums = attend(query_three, pair_whole, place_here, place_all)
    else:
        attended, log_sums = lax.fori_loop(
            0,
            seq_count * heads_here,
            forward_item,
            (
                jnp.zeros((seq_count, seq_rows, columns), jnp.float32),
                jnp.zeros((seq_count, seq_rows, heads_here), jnp.float32),
            ),
        )
        mixed_flip = attended.reshape(total_rows, columns).astype(jnp.bfloat16).T
    all_mixed = lax.all_gather(mixed_flip, "tp", axis=0, tiled=True)
    attn_out = jnp.einsum("ht,hd->td", all_mixed, all_out, preferred_element_type=jnp.float32) + out_bias
    middle = inputs + attn_out
    normed_two, scale_two = normalized(middle)
    act_two = (normed_two * ln2_gain + ln2_bias).astype(jnp.bfloat16)
    hidden_pre = jnp.dot(act_two, whole_fc, preferred_element_type=jnp.float32) + fc_bias
    hidden_out, gelu_back = jax.vjp(gelu_curve, hidden_pre)
    hidden = hidden_out.astype(jnp.bfloat16)
    branch_part = jnp.einsum(
        "tf,df->td", hidden, proj_flip, preferred_element_type=jnp.float32
    ).astype(jnp.bfloat16)
    upstream_low = out_grad.reshape(total_rows, model_width)
    upstream = upstream_low.astype(jnp.float32)
    proj_bias_grad = jnp.sum(upstream, axis=0)
    proj_grad = jnp.einsum("td,tf->df", upstream_low, hidden, preferred_element_type=jnp.float32)
    hidden_grad = jnp.dot(upstream_low, proj_flip, preferred_element_type=jnp.float32)
    pre_grad = gelu_back(hidden_grad)[0].astype(jnp.bfloat16)
    fc_bias_grad = jnp.sum(pre_grad.astype(jnp.float32), axis=0)
    fc_grad = jnp.einsum("td,tf->df", act_two, pre_grad, preferred_element_type=jnp.float32)
    act_two_part = jnp.einsum("tf,df->td", pre_grad, whole_fc, preferred_element_type=jnp.float32)
    ln2_gain_grad = jnp.sum(act_two_part * normed_two, axis=0)
    ln2_bias_grad = jnp.sum(act_two_part, axis=0)
    act_two_grad = lax.psum(act_two_part.astype(jnp.bfloat16), "tp").astype(jnp.float32)
    act_two_grad, branch_part = lax.optimization_barrier((act_two_grad, branch_part))
    branch_low = lax.psum(branch_part, "tp")
    shards = combine(scatter_rows(jnp.stack([fc_grad, proj_grad]), "fsdp"))
    shard_fc, shard_proj = shards[0], shards[1].T
    middle_grad = upstream + norm_back(act_two_grad, ln2_gain, normed_two, scale_two)
    attn_grad = middle_grad.astype(jnp.bfloat16)
    out_bias_grad = jnp.sum(attn_grad.astype(jnp.float32), axis=0)
    out_flip_grad = jnp.einsum("td,ht->dh", attn_grad, mixed_flip, preferred_element_type=jnp.float32)
    mixed_grad = (
        jnp.einsum("td,hd->th", attn_grad, whole_out, preferred_element_type=jnp.float32)
        .astype(jnp.bfloat16)
        .reshape(seq_count, seq_rows, columns)
    )
    if in_kernel:
        query_grad_low, pair_terms = attend_back(
            query_three, pair_whole, mixed_grad, log_sums, place_here, place_all
        )
        query_grad_low = query_grad_low.reshape(total_rows, columns)
    else:
        query_grads = []
        pair_grads = []
        for sequence in range(seq_count):
            query_grad, pair_term, delta_cols = query_side(
                query_three[sequence],
                pair_whole[sequence],
                mixed_grad[sequence],
                log_sums[sequence],
                visible,
            )
            query_grads.append(query_grad)
            pair_grads.append(pair_term)
        query_grad_low = jnp.concatenate(query_grads, axis=0).astype(jnp.bfloat16)
        pair_terms = jnp.stack(pair_grads)
    if exchanged:
        given = swap(pair_terms[:, seq_rows:].astype(jnp.bfloat16), "ctx", 1)
        pair_sums = pair_terms[:, :seq_rows] + given.astype(jnp.float32)
    else:
        pair_sums = scatter_rows(pair_terms, "ctx")
    pair_low = pair_sums.astype(jnp.bfloat16).reshape(total_rows, 2 * columns)
    stacked = jnp.stack([query_grad_low, pair_low[:, :columns], pair_low[:, columns:]])
    qv_bias_grad = jnp.stack(
        [
            jnp.sum(stacked[0].astype(jnp.float32), axis=0),
            jnp.sum(stacked[2].astype(jnp.float32), axis=0),
        ]
    )
    qkv_grad = jnp.einsum("td,cth->cdh", act_one, stacked, preferred_element_type=jnp.float32)
    act_one_part = jnp.einsum("cth,cdh->td", stacked, whole_qkv, preferred_element_type=jnp.float32)
    ln1_gain_grad = jnp.sum(act_one_part * normed_one, axis=0)
    ln1_bias_grad = jnp.sum(act_one_part, axis=0)
    branch_low, act_one_low = lax.optimization_barrier(
        (branch_low, act_one_part.astype(jnp.bfloat16))
    )
    act_one_grad = lax.psum(act_one_low, "tp").astype(jnp.float32)
    shards = combine(scatter_rows(jnp.concatenate([qkv_grad, out_flip_grad[None]]), "fsdp"))
    shard_qkv, shard_out = shards[:3], shards[3].T
    norm_sums = sum_all(
        jnp.concatenate([ln1_gain_grad, ln1_bias_grad, ln2_gain_grad, ln2_bias_grad]), "tp"
    )
    packed = jnp.concatenate(
        [norm_sums, out_bias_grad, proj_bias_grad, fc_bias_grad, qv_bias_grad[0], qv_bias_grad[1]]
    )
    packed = sum_all(sum_all(packed, "fsdp"), "ctx")
    result = (
        (middle + (branch_low.astype(jnp.float32) + proj_bias))
        .astype(jnp.bfloat16)
        .reshape(seq_count, seq_rows, model_width)
    )
    act_one_grad, packed, shard_qkv, shard_out = lax.optimization_barrier(
        (act_one_grad, packed, shard_qkv, shard_out)
    )
    tokens_grad = (middle_grad + norm_back(act_one_grad, ln1_gain, normed_one, scale_one)).reshape(
        seq_count, seq_rows, model_width
    )
    hidden_here = fc_bias_grad.shape[0]
    norm_sums = packed[: 6 * model_width].reshape(6, model_width)
    fc_bias_sum = packed[6 * model_width : 6 * model_width + hidden_here]
    qv_sum = packed[6 * model_width + hidden_here :].reshape(2, columns)
    return (
        result,
        tokens_grad,
        norm_sums[0],
        norm_sums[1],
        shard_qkv,
        qv_sum,
        shard_out,
        norm_sums[4],
        norm_sums[2],
        norm_sums[3],
        shard_fc,
        fc_bias_sum,
        shard_proj,
        norm_sums[5],
    )


def solution(mesh):
    in_specs = (
        P("fsdp", "ctx", None),
        P(),
        P(),
        P(None, "fsdp", "tp"),
        P(None, "tp"),
        P("tp", "fsdp"),
        P(),
        P(),
        P(),
        P("fsdp", "tp"),
        P("tp"),
        P("tp", "fsdp"),
        P(),
        P(),
        P("fsdp", "ctx", None),
    )
    out_specs = (
        P("fsdp", "ctx", None),
        P("fsdp", "ctx", None),
        P(),
        P(),
        P(None, "fsdp", "tp"),
        P(None, "tp"),
        P("tp", "fsdp"),
        P(),
        P(),
        P(),
        P("fsdp", "tp"),
        P("tp"),
        P("tp", "fsdp"),
        P(),
    )
    return jax.shard_map(body, mesh=mesh, in_specs=in_specs, out_specs=out_specs, check_vma=False)
```
